512 devices in a mesh: loop: 64 (over z, x_hi, core), narrow: 8 (over x_lo, y).
Axes of the slice: x: 4 (x_hi: 2, x_lo: 2; x = x_hi * 2 + x_lo), y: 4, z: 16, core: 2. Of those that a mesh axis runs over, the one named last changes fastest.
Arguments:
- tokens: bfloat16 [1024, 8192], P('loop', 'narrow'), may hold values from -6 to 6
- gate_weight: bfloat16 [8192, 28672], P('narrow', 'loop'), may hold values from -0.0625 to 0.0625
- up_weight: bfloat16 [8192, 28672], P('narrow', 'loop'), may hold values from -0.0625 to 0.0625
- down_weight: bfloat16 [28672, 8192], P('loop', 'narrow'), may hold values from -0.03125 to 0.03125
Outputs:
- mixed: bfloat16 [1024, 8192], P('loop', 'narrow')
The draws below stay inside these ranges and needn't reach their ends.
All inputs are finite; a program needn't handle non-finite values.
Results may differ from the reference program's by a relative error of at most 0.0049.
Values may be sent and summed in bfloat16 or wider, within the bound.
No kernel may reach another device: no remote copies, remote signals or barrier semaphores. Data moves between devices by JAX's collectives and lax.ppermute only.
A program may use at most 64 MiB of HBM per device.

```python
import jax
import jax.numpy as jnp

D = 8192
FF = 28672
TOK = 1024


def block_levels(own_key, dims, cuts, least, top_value):
    factor_of, own = 1.0, jax.random.fold_in(own_key, 6)
    for axis_at, parts in cuts:
        steps = jnp.exp(jax.random.uniform(jax.random.fold_in(own, axis_at), (parts,), jnp.float32, least / len(cuts), top_value / len(cuts)))
        factor_of = factor_of * jnp.repeat(steps, dims[axis_at] // parts).reshape([-1 if axis == axis_at else 1 for axis in range(len(dims))])
    return factor_of


def noise(stream_key, shape, width, reach, shards=(), kind=jnp.bfloat16):
    loudness = block_levels(stream_key, shape, shards, -0.22, 0.18) if shards else 1.0
    drawn = jax.random.normal(stream_key, shape, jnp.float32) * width * loudness
    return jnp.minimum(jnp.maximum(drawn, -reach), reach).astype(kind)


def setup_inputs(seed: int = 0) -> dict:
    key_list = jax.random.split(jax.random.key(seed), 5)
    return {
        "tokens": noise(key_list[0], (TOK, D), 1.0, 6.0, ((0, 64), (1, 8))),
        "gate_weight": noise(key_list[1], (D, FF), D ** -0.5, 0.0625, ((0, 8), (1, 64))),
        "up_weight": noise(key_list[2], (D, FF), D ** -0.5, 0.0625, ((0, 8), (1, 64))),
        "down_weight": noise(key_list[3], (FF, D), FF ** -0.5, 0.03125, ((0, 64), (1, 8))),
    }


def reference(tokens, gate_weight, up_weight, down_weight):
    gate = jnp.dot(tokens, gate_weight, preferred_element_type=jnp.float32)
    up = jnp.dot(tokens, up_weight, preferred_element_type=jnp.float32)
    hidden = (jax.nn.silu(gate) * up).astype(jnp.bfloat16)
    return jnp.dot(hidden, down_weight, preferred_element_type=jnp.float32).astype(jnp.bfloat16)
```

```python
import jax
import jax.numpy as jnp
from jax import lax
from jax.sharding import Mesh, PartitionSpec as P

AXES = ("zh", "zl", "xh", "core", "xl", "y")
Z = ("zh", "zl")
NARROW = ("xl", "y")
SWAP = [(0, 1), (1, 0)]


def f32dot(a, b):
    return jnp.dot(a, b, preferred_element_type=jnp.float32)


def shards(tokens, gate_weight, up_weight, down_weight):
    gate_other = lax.ppermute(gate_weight, "core", SWAP)
    up_other = lax.ppermute(up_weight, "core", SWAP)
    down_other = lax.ppermute(down_weight, "core", SWAP)

    rows = lax.all_gather(tokens, Z, axis=0, tiled=True)
    near = lax.all_to_all(jnp.broadcast_to(rows, (2, *rows.shape)), "xh", 0, 0)
    rows = near.reshape(-1, tokens.shape[1])
    n_rows = rows.shape[0]

    gates = jnp.concatenate((gate_weight, gate_other), axis=1)
    ups = jnp.concatenate((up_weight, up_other), axis=1)
    width = gates.shape[1]
    partial = jnp.concatenate(
        (f32dot(rows, gates).astype(jnp.bfloat16), f32dot(rows, ups).astype(jnp.bfloat16)), axis=1
    )
    partial = partial.reshape(8, n_rows // 8, 2 * width)
    parts = lax.all_to_all(partial, NARROW, 0, 0)
    totals = jnp.sum(parts.astype(jnp.float32), axis=0)
    hidden = (jax.nn.silu(totals[:, :width]) * totals[:, width:]).astype(jnp.bfloat16)
    hidden = lax.all_to_all(jnp.broadcast_to(hidden, (8, *hidden.shape)), NARROW, 0, 0)
    hidden = hidden.reshape(n_rows, width)

    downs = jnp.concatenate((down_weight, down_other), axis=0)
    mixed = f32dot(hidden, downs).astype(jnp.bfloat16)
    mixed = mixed.reshape(2, 4, 4, 16, -1)
    mixed = mixed.transpose(2, 0, 1, 3, 4).reshape(8, 64, -1)
    mixed = lax.all_to_all(mixed, ("zl", "xh"), 0, 0)
    mixed = jnp.sum(mixed.astype(jnp.float32), axis=0).astype(jnp.bfloat16)
    mixed = lax.all_to_all(mixed.reshape(4, 16, -1), "zh", 0, 0)
    return jnp.sum(mixed.astype(jnp.float32), axis=0).astype(jnp.bfloat16)


def solution(mesh):
    fine = Mesh(mesh.devices.reshape(4, 4, 2, 2, 2, 4), AXES)
    loop, narrow = ("zh", "zl", "xh", "core"), NARROW
    return jax.shard_map(
        shards,
        mesh=fine,
        in_specs=(P(loop, narrow), P(narrow, loop), P(narrow, loop), P(loop, narrow)),
        out_specs=P(loop, narrow),
        check_vma=False,
    )
```

```python
import jax
import jax.numpy as jnp
from jax import lax
from jax.experimental import pallas as pl
from jax.experimental.pallas import tpu as pltpu
from jax.sharding import Mesh, PartitionSpec as P

AXES = ("zh", "za", "zb", "xh", "core", "xl", "y")
NARROW = ("xl", "y")
SWAP = [(0, 1), (1, 0)]
VMEM = pl.BlockSpec(memory_space=pltpu.VMEM)
SMEM = pl.BlockSpec(memory_space=pltpu.SMEM)


def total(parts):
    return jnp.sum(parts.astype(jnp.float32), axis=0)


def matmul(a, b, b_dim):
    return lax.dot_general(a, b, (((1,), (b_dim,)), ((), ())), preferred_element_type=jnp.float32)


def own_kernel(x_ref, *refs):
    *weight_refs, out_ref = refs
    width = weight_refs[0].shape[0]
    for i, w_ref in enumerate(weight_refs):
        product = matmul(x_ref[...], w_ref[...], 1)
        out_ref[:, i * width : (i + 1) * width] = product.astype(out_ref.dtype)


def join_kernel(at_xh_ref, x_ref, own_ref, *refs):
    *weight_refs, out_ref = refs
    width = weight_refs[0].shape[0]
    at_xh = at_xh_ref[0]

    def put(slot, columns, block):
        for at in range(16):
            high, low, za, zb = at // 8, at // 4 % 2, at // 2 % 2, at % 2
            out_ref[za, slot, high, zb, low, :, columns] = block[at * 16 : (at + 1) * 16]

    for i, w_ref in enumerate(weight_refs):
        columns = slice(i * width, (i + 1) * width)
        put(1 - at_xh, columns, matmul(x_ref[...], w_ref[...], 1).astype(out_ref.dtype))
    put(at_xh, slice(None), own_ref[...])


def down_kernel(at_zb_ref, hidden_ref, *refs):
    *weight_refs, out_ref, joined_ref = refs
    width = weight_refs[0].shape[0]
    at_zb = at_zb_ref[0]
    for i, w_ref in enumerate(weight_refs):
        joined_ref[i // 2, i % 2 * width : (i % 2 + 1) * width] = w_ref[...]
    mixed = matmul(hidden_ref[at_zb], joined_ref[0], 0)
    mixed = mixed + matmul(hidden_ref[1 - at_zb], joined_ref[1], 0)
    out_ref[...] = mixed.astype(out_ref.dtype)


def call(kernel, specs, out_shape, flops, *args, scratch=()):
    return pl.pallas_call(
        kernel,
        out_shape=jax.ShapeDtypeStruct(out_shape, jnp.bfloat16),
        in_specs=specs,
        out_specs=VMEM,
        scratch_shapes=scratch,
        cost_estimate=pl.CostEstimate(
            flops=flops, bytes_accessed=2 * sum(a.size for a in args), transcendentals=0
        ),
        compiler_params=pltpu.CompilerParams(vmem_limit_bytes=32 << 20),
    )(*args)


def shards(tokens, gate_weight, up_weight, down_weight):
    depth = tokens.shape[1]
    at_xh = lax.axis_index("xh").reshape(1)
    at_zb = lax.axis_index("zb").reshape(1)
    gate, up = gate_weight.T, up_weight.T
    width = gate.shape[0]
    weights = [gate, lax.ppermute(gate, "core", SWAP), up, lax.ppermute(up, "core", SWAP)]

    rows = lax.all_gather(tokens, ("zh", "za", "zb"), axis=0, tiled=True)
    n_rows = rows.shape[0]
    other_rows = lax.ppermute(rows, "xh", SWAP)
    flops = 8 * n_rows * depth * width
    own = call(own_kernel, [VMEM] * 5, (n_rows, 4 * width), flops, rows, *weights)
    partial = call(
        join_kernel,
        [SMEM] + [VMEM] * 6,
        (2, 2, 2, 2, 2, 16, 4 * width),
        flops,
        at_xh,
        other_rows,
        own,
        *weights,
    )
    down_weight, partial = lax.optimization_barrier((down_weight, partial))
    down_far = lax.ppermute(down_weight, "zb", SWAP)
    parts = lax.all_to_all(partial.reshape(8, 2, 32, 4 * width), NARROW, 0, 0)
    parts, down_weight, down_far = lax.optimization_barrier((parts, down_weight, down_far))
    downs = [down_weight, lax.ppermute(down_weight, "core", SWAP)]
    downs += [down_far, lax.ppermute(down_far, "core", SWAP)]

    totals = total(parts)
    hidden = (jax.nn.silu(totals[..., : 2 * width]) * totals[..., 2 * width :]).astype(jnp.bfloat16)
    hidden = jnp.broadcast_to(hidden[:, None], (2, 8, 32, 2 * width)).reshape(16, 32, 2 * width)
    hidden = lax.all_to_all(hidden, ("zb", *NARROW), 0, 0).reshape(2, n_rows, 2 * width)
    mixed = call(
        down_kernel,
        [SMEM] + [VMEM] * 5,
        (n_rows, depth),
        8 * n_rows * depth * width,
        at_zb,
        hidden,
        *downs,
        scratch=[pltpu.VMEM((2, 2 * width, depth), jnp.bfloat16)],
    )
    mixed = total(lax.all_to_all(mixed.reshape(4, 64, depth), ("za", "xh"), 0, 0))
    mixed = lax.all_to_all(mixed.astype(jnp.bfloat16).reshape(4, 16, depth), "zh", 0, 0)
    return total(mixed).astype(jnp.bfloat16)


def solution(mesh):
    fine = Mesh(mesh.devices.reshape(4, 2, 2, 2, 2, 2, 4), AXES)
    loop = ("zh", "za", "zb", "xh", "core")
    return jax.shard_map(
        shards,
        mesh=fine,
        in_specs=(P(loop, NARROW), P(NARROW, loop), P(NARROW, loop), P(loop, NARROW)),
        out_specs=P(loop, NARROW),
        check_vma=False,
    )
```

```python
import jax
import jax.numpy as jnp
from jax import lax
from jax.experimental import pallas as pl
from jax.experimental.pallas import tpu as pltpu
from jax.sharding import Mesh, PartitionSpec as P

AXES = ("zh", "za", "zb", "xh", "core", "xl", "y")
NARROW = ("xl", "y")
SWAP = [(0, 1), (1, 0)]
VMEM = pl.BlockSpec(memory_space=pltpu.VMEM)
SMEM = pl.BlockSpec(memory_space=pltpu.SMEM)


def total(parts):
    return jnp.sum(parts.astype(jnp.float32), axis=0)


def matmul(a, b, b_dim):
    return lax.dot_general(a, b, (((1,), (b_dim,)), ((), ())), preferred_element_type=jnp.float32)


def own_kernel(x_ref, *refs):
    *weight_refs, out_ref = refs
    width = weight_refs[0].shape[0]
    for i, w_ref in enumerate(weight_refs):
        product = matmul(x_ref[...], w_ref[...], 1)
        out_ref[:, i * width : (i + 1) * width] = product.astype(out_ref.dtype)


def join_kernel(at_xh_ref, x_ref, own_ref, *refs):
    *weight_refs, out_ref = refs
    width = weight_refs[0].shape[0]
    at_xh = at_xh_ref[0]

    def put(slot, columns, block):
        for at in range(16):
            high, low, za, zb = at // 8, at // 4 % 2, at // 2 % 2, at % 2
            out_ref[za, slot, high, zb, low, :, columns] = block[at * 16 : (at + 1) * 16]

    for i, w_ref in enumerate(weight_refs):
        columns = slice(i * width, (i + 1) * width)
        put(1 - at_xh, columns, matmul(x_ref[...], w_ref[...], 1).astype(out_ref.dtype))
    put(at_xh, slice(None), own_ref[...])


def hidden_kernel(parts_ref, out_ref):
    width = out_ref.shape[-1]
    totals = parts_ref[0].astype(jnp.float32)
    for i in range(1, parts_ref.shape[0]):
        totals = totals + parts_ref[i].astype(jnp.float32)
    hidden = (jax.nn.silu(totals[..., :width]) * totals[..., width:]).astype(out_ref.dtype)
    for i in range(out_ref.shape[1]):
        out_ref[:, i] = hidden


def down_kernel(at_zb_ref, hidden_ref, *refs):
    *weight_refs, out_ref, joined_ref = refs
    width = weight_refs[0].shape[0]
    at_zb = at_zb_ref[0]
    for i, w_ref in enumerate(weight_refs):
        joined_ref[i // 2, i % 2 * width : (i % 2 + 1) * width] = w_ref[...]
    mixed = matmul(hidden_ref[at_zb], joined_ref[0], 0)
    mixed = mixed + matmul(hidden_ref[1 - at_zb], joined_ref[1], 0)
    out_ref[...] = mixed.astype(out_ref.dtype)


def call(kernel, specs, out_shape, flops, *args, scratch=()):
    return pl.pallas_call(
        kernel,
        out_shape=jax.ShapeDtypeStruct(out_shape, jnp.bfloat16),
        in_specs=specs,
        out_specs=VMEM,
        scratch_shapes=scratch,
        cost_estimate=pl.CostEstimate(
            flops=flops, bytes_accessed=2 * sum(a.size for a in args), transcendentals=0
        ),
        compiler_params=pltpu.CompilerParams(vmem_limit_bytes=16 << 20),
    )(*args)


def shards(tokens, gate_weight, up_weight, down_weight):
    depth = tokens.shape[1]
    at_xh = lax.axis_index("xh").reshape(1)
    at_zb = lax.axis_index("zb").reshape(1)
    gate, up = gate_weight.T, up_weight.T
    width = gate.shape[0]
    weights = [gate, lax.ppermute(gate, "core", SWAP), up, lax.ppermute(up, "core", SWAP)]

    rows = lax.all_gather(tokens, ("zh", "za", "zb"), axis=0, tiled=True)
    n_rows = rows.shape[0]
    other_rows = lax.ppermute(rows, "xh", SWAP)
    flops = 8 * n_rows * depth * width
    own = call(own_kernel, [VMEM] * 5, (n_rows, 4 * width), flops, rows, *weights)
    partial = call(
        join_kernel,
        [SMEM] + [VMEM] * 6,
        (2, 2, 2, 2, 2, 16, 4 * width),
        flops,
        at_xh,
        other_rows,
        own,
        *weights,
    )
    down_weight, partial = lax.optimization_barrier((down_weight, partial))
    down_far = lax.ppermute(down_weight, "zb", SWAP)
    down_core = lax.ppermute(down_weight, "core", SWAP)
    parts = lax.all_to_all(partial.reshape(8, 2, 32, 4 * width), NARROW, 0, 0)
    hidden = call(hidden_kernel, [VMEM], (2, 8, 32, 2 * width), 16 * 64 * 4 * width, parts)
    hidden, down_core, down_far = lax.optimization_barrier((hidden, down_core, down_far))
    downs = [down_weight, down_core, down_far, lax.ppermute(down_far, "core", SWAP)]
    hidden = lax.all_to_all(hidden.reshape(16, 32, 2 * width), ("zb", *NARROW), 0, 0)
    hidden = hidden.reshape(2, n_rows, 2 * width)
    mixed = call(
        down_kernel,
        [SMEM] + [VMEM] * 5,
        (n_rows, depth),
        8 * n_rows * depth * width,
        at_zb,
        hidden,
        *downs,
        scratch=[pltpu.VMEM((2, 2 * width, depth), jnp.bfloat16)],
    )
    mixed = total(lax.all_to_all(mixed.reshape(4, 64, depth), ("za", "xh"), 0, 0))
    mixed = lax.all_to_all(mixed.astype(jnp.bfloat16).reshape(4, 16, depth), "zh", 0, 0)
    return total(mixed).astype(jnp.bfloat16)


def solution(mesh):
    fine = Mesh(mesh.devices.reshape(4, 2, 2, 2, 2, 2, 4), AXES)
    loop = ("zh", "za", "zb", "xh", "core")
    return jax.shard_map(
        shards,
        mesh=fine,
        in_specs=(P(loop, NARROW), P(NARROW, loop), P(NARROW, loop), P(loop, NARROW)),
        out_specs=P(loop, NARROW),
        check_vma=False,
    )
```

```python
import jax
import jax.numpy as jnp
from jax import lax
from jax.experimental import pallas as pl
from jax.experimental.pallas import tpu as pltpu
from jax.sharding import Mesh, PartitionSpec as P

AXES = ("zh", "za", "zb", "xh", "core", "xl", "y")
NARROW = ("xl", "y")
SWAP = [(0, 1), (1, 0)]
VMEM = pl.BlockSpec(memory_space=pltpu.VMEM)
SMEM = pl.BlockSpec(memory_space=pltpu.SMEM)
HBM = pl.BlockSpec(memory_space=pltpu.HBM)


def total(parts):
    return jnp.sum(parts.astype(jnp.float32), axis=0)


def matmul(a, b, b_dim):
    return lax.dot_general(a, b, (((1,), (b_dim,)), ((), ())), preferred_element_type=jnp.float32)


def project_kernel(slot_ref, x_ref, *refs):
    out_ref, block_ref, sems = refs[-3:]
    weight_refs = refs[:4]
    width = weight_refs[0].shape[0]
    copies = []
    for i, w_ref in enumerate(weight_refs):
        product = matmul(x_ref[...], w_ref[...], 1).astype(out_ref.dtype)
        columns = slice(i * width, (i + 1) * width)
        for at in range(16):
            high, low, za, zb = at // 8, at // 4 % 2, at // 2 % 2, at % 2
            block_ref[za, high, zb, low, :, columns] = product[at * 16 : (at + 1) * 16]
        if i % 2:
            half = pl.ds((i - 1) * width, 2 * width)
            copies.append(
                pltpu.make_async_copy(
                    block_ref.at[..., half],
                    out_ref.at[slot_ref[0], :, :, :, :, :, half],
                    sems.at[i // 2],
                )
            )
            copies[-1].start()
    for copy in copies:
        copy.wait()


def hidden_kernel(parts_ref, out_ref):
    width = out_ref.shape[-1]
    totals = parts_ref[0].astype(jnp.float32)
    for i in range(1, parts_ref.shape[0]):
        totals = totals + parts_ref[i].astype(jnp.float32)
    hidden = (jax.nn.silu(totals[..., :width]) * totals[..., width:]).astype(out_ref.dtype)
    for i in range(out_ref.shape[0]):
        out_ref[i] = hidden


def down_kernel(at_zb_ref, hidden_ref, *refs):
    *weight_refs, out_ref = refs
    width = weight_refs[0].shape[0]
    at_zb = at_zb_ref[0]
    mixed = 0.0
    for i, w_ref in enumerate(weight_refs):
        units = hidden_ref[:, at_zb if i < 2 else 1 - at_zb, :, i % 2 * width : (i % 2 + 1) * width]
        mixed = mixed + matmul(units.reshape(out_ref.shape[0], width), w_ref[...], 0)
    out_ref[...] = mixed.astype(out_ref.dtype)


def call(kernel, specs, out_shape, flops, *args, out_spec=VMEM, scratch=(), aliases={}):
    return pl.pallas_call(
        kernel,
        out_shape=jax.ShapeDtypeStruct(out_shape, jnp.bfloat16),
        in_specs=specs,
        out_specs=out_spec,
        input_output_aliases=aliases,
        scratch_shapes=scratch,
        cost_estimate=pl.CostEstimate(
            flops=flops, bytes_accessed=2 * sum(a.size for a in args), transcendentals=0
        ),
        compiler_params=pltpu.CompilerParams(vmem_limit_bytes=16 << 20),
    )(*args)


def shards(tokens, gate_weight, up_weight, down_weight):
    depth = tokens.shape[1]
    at_xh = lax.axis_index("xh").reshape(1)
    at_zb = lax.axis_index("zb").reshape(1)
    gate, up = gate_weight.T, up_weight.T
    width = gate.shape[0]
    weights = [gate, lax.ppermute(gate, "core", SWAP), up, lax.ppermute(up, "core", SWAP)]

    rows = lax.all_gather(tokens, ("zh", "za", "zb"), axis=0, tiled=True)
    n_rows = rows.shape[0]
    other_rows = lax.ppermute(rows, "xh", SWAP)
    flops = 8 * n_rows * depth * width

    def project(slot, x, *started):
        return call(
            project_kernel,
            [SMEM] + [VMEM] * 5 + [HBM] * len(started),
            (2, 2, 2, 2, 2, 16, 4 * width),
            flops,
            slot,
            x,
            *weights,
            *started,
            out_spec=HBM,
            scratch=[
                pltpu.VMEM((2, 2, 2, 2, 16, 4 * width), jnp.bfloat16),
                pltpu.SemaphoreType.DMA((2,)),
            ],
            aliases={6: 0} if started else {},
        )

    partial = project(1 - at_xh, other_rows, project(at_xh, rows))
    down_weight, partial = lax.optimization_barrier((down_weight, partial))
    down_far = lax.ppermute(down_weight, "zb", SWAP)
    down_core = lax.ppermute(down_weight, "core", SWAP)
    parts = lax.all_to_all(partial.reshape(8, 2, 32, 4 * width), NARROW, 0, 0)
    hidden = call(hidden_kernel, [VMEM], (8, 2, 32, 2 * width), 16 * 64 * 4 * width, parts)
    hidden, down_core, down_far = lax.optimization_barrier((hidden, down_core, down_far))
    downs = [down_weight, down_core, down_far, lax.ppermute(down_far, "core", SWAP)]
    hidden = lax.all_to_all(hidden.reshape(16, 32, 2 * width), (*NARROW, "zb"), 0, 0)
    hidden = hidden.reshape(8, 2, 32, 2 * width)
    mixed = call(
        down_kernel,
        [SMEM] + [VMEM] * 5,
        (n_rows, depth),
        8 * n_rows * depth * width,
        at_zb,
        hidden,
        *downs,
    )
    mixed = total(lax.all_to_all(mixed.reshape(4, 64, depth), ("xh", "za"), 0, 0))
    mixed = lax.all_to_all(mixed.astype(jnp.bfloat16).reshape(4, 16, depth), "zh", 0, 0)
    return total(mixed).astype(jnp.bfloat16)


def solution(mesh):
    fine = Mesh(mesh.devices.reshape(4, 2, 2, 2, 2, 2, 4), AXES)
    loop = ("zh", "za", "zb", "xh", "core")
    return jax.shard_map(
        shards,
        mesh=fine,
        in_specs=(P(loop, NARROW), P(NARROW, loop), P(NARROW, loop), P(loop, NARROW)),
        out_specs=P(loop, NARROW),
        check_vma=False,
    )
```

```python
import jax
import jax.numpy as jnp
from jax import lax
from jax.experimental import pallas as pl
from jax.experimental.pallas import tpu as pltpu
from jax.sharding import Mesh, PartitionSpec as P

AXES = ("zh", "za", "zb", "xh", "core", "xl", "y")
NARROW = ("xl", "y")
SWAP = [(0, 1), (1, 0)]
LOOP = ("zh", "za", "zb", "xh", "core")
GROUPS = ((0, 3, 6, 1), (7, 4, 5, 2))


def loop_at(pair, zb, xh, core):
    return pair * 8 + zb * 4 + xh * 2 + core


NEAR = [
    [loop_at(group[at], zb, xh, core) for xh in range(2) for group in GROUPS]
    for at in range(4)
    for zb in range(2)
    for core in range(2)
]
FAR = [
    [loop_at(pair, zb, xh, core) for pair in group]
    for group in GROUPS
    for zb in range(2)
    for xh in range(2)
    for core in range(2)
]
VMEM = pl.BlockSpec(memory_space=pltpu.VMEM)
SMEM = pl.BlockSpec(memory_space=pltpu.SMEM)
HBM = pl.BlockSpec(memory_space=pltpu.HBM)


def total(parts):
    return jnp.sum(parts.astype(jnp.float32), axis=0)


def matmul(a, b, b_dim):
    return lax.dot_general(a, b, (((1,), (b_dim,)), ((), ())), preferred_element_type=jnp.float32)


def project_kernel(slot_ref, x_ref, *refs):
    out_ref, block_ref, sems = refs[-3:]
    weight_refs = refs[:4]
    width = weight_refs[0].shape[0]
    copies = []
    for i, w_ref in enumerate(weight_refs):
        product = matmul(x_ref[...], w_ref[...], 1).astype(out_ref.dtype)
        columns = slice(i * width, (i + 1) * width)
        for at in range(16):
            za = int(at // 2 in GROUPS[1])
            place, zb = GROUPS[za].index(at // 2), at % 2
            block_ref[za, place // 2, zb, place % 2, :, columns] = product[at * 16 : (at + 1) * 16]
        if i % 2:
            half = pl.ds((i - 1) * width, 2 * width)
            copies.append(
                pltpu.make_async_copy(
                    block_ref.at[..., half],
                    out_ref.at[slot_ref[0], :, :, :, :, :, half],
                    sems.at[i // 2],
                )
            )
            copies[-1].start()
    for copy in copies:
        copy.wait()


def hidden_kernel(parts_ref, out_ref):
    width = out_ref.shape[-1]
    totals = parts_ref[0].astype(jnp.float32)
    for i in range(1, parts_ref.shape[0]):
        totals = totals + parts_ref[i].astype(jnp.float32)
    hidden = (jax.nn.silu(totals[..., :width]) * totals[..., width:]).astype(out_ref.dtype)
    for i in range(out_ref.shape[0]):
        out_ref[i] = hidden


def down_kernel(at_zb_ref, hidden_ref, *refs):
    *weight_refs, out_ref, fetched_ref, sems = refs
    width = weight_refs[0].shape[0]
    at_zb = at_zb_ref[0]
    copies = [
        pltpu.make_async_copy(weight_refs[1 + i], fetched_ref.at[i], sems.at[i]) for i in range(2)
    ]
    for copy in copies:
        copy.start()
    mixed = 0.0
    for i in (0, 3, 1, 2):
        side = at_zb if i < 2 else 1 - at_zb
        units = hidden_ref[:, side, :, i % 2 * width : (i % 2 + 1) * width]
        if i in (1, 2):
            copies[i - 1].wait()
        weight = fetched_ref[i - 1] if i in (1, 2) else weight_refs[i][...]
        mixed = mixed + matmul(units.reshape(out_ref.shape[0], width), weight, 0)
    out_ref[...] = mixed.astype(out_ref.dtype)


def call(kernel, specs, out_shape, flops, *args, out_spec=VMEM, scratch=(), aliases={}):
    return pl.pallas_call(
        kernel,
        out_shape=jax.ShapeDtypeStruct(out_shape, jnp.bfloat16),
        in_specs=specs,
        out_specs=out_spec,
        input_output_aliases=aliases,
        scratch_shapes=scratch,
        cost_estimate=pl.CostEstimate(
            flops=flops, bytes_accessed=2 * sum(a.size for a in args), transcendentals=0
        ),
        compiler_params=pltpu.CompilerParams(vmem_limit_bytes=16 << 20),
    )(*args)


def shards(tokens, gate_weight, up_weight, down_weight):
    depth = tokens.shape[1]
    at_xh = lax.axis_index("xh").reshape(1)
    at_zb = lax.axis_index("zb").reshape(1)
    gate, up = gate_weight.T, up_weight.T
    width = gate.shape[0]
    weights = [gate, lax.ppermute(gate, "core", SWAP), up, lax.ppermute(up, "core", SWAP)]

    rows = lax.all_gather(tokens, ("zh", "za", "zb"), axis=0, tiled=True)
    n_rows = rows.shape[0]
    other_rows = lax.ppermute(rows, "xh", SWAP)
    flops = 8 * n_rows * depth * width

    def project(slot, x, *started):
        return call(
            project_kernel,
            [SMEM] + [VMEM] * 5 + [HBM] * len(started),
            (2, 2, 2, 2, 2, 16, 4 * width),
            flops,
            slot,
            x,
            *weights,
            *started,
            out_spec=HBM,
            scratch=[
                pltpu.VMEM((2, 2, 2, 2, 16, 4 * width), jnp.bfloat16),
                pltpu.SemaphoreType.DMA((2,)),
            ],
            aliases={6: 0} if started else {},
        )

    partial = project(1 - at_xh, other_rows, project(at_xh, rows))
    down_weight, partial = lax.optimization_barrier((down_weight, partial))
    down_far = lax.ppermute(down_weight, "zb", SWAP)
    down_core = lax.ppermute(down_weight, "core", SWAP)
    parts = lax.all_to_all(partial.reshape(8, 2, 32, 4 * width), NARROW, 0, 0)
    hidden = call(hidden_kernel, [VMEM], (8, 2, 32, 2 * width), 16 * 64 * 4 * width, parts)
    hidden, down_core, down_far = lax.optimization_barrier((hidden, down_core, down_far))
    downs = [down_weight, down_core, down_far, lax.ppermute(down_far, "core", SWAP)]
    hidden = lax.all_to_all(hidden.reshape(16, 32, 2 * width), (*NARROW, "zb"), 0, 0)
    hidden = hidden.reshape(8, 2, 32, 2 * width)
    mixed = call(
        down_kernel,
        [SMEM, VMEM, VMEM, HBM, HBM, VMEM],
        (n_rows, depth),
        8 * n_rows * depth * width,
        at_zb,
        hidden,
        *downs,
        scratch=[
            pltpu.VMEM((2, width, depth), jnp.bfloat16),
            pltpu.SemaphoreType.DMA((2,)),
        ],
    )
    mixed = total(lax.all_to_all(mixed.reshape(4, 64, depth), LOOP, 0, 0, axis_index_groups=NEAR))
    mixed = lax.all_to_all(mixed.astype(jnp.bfloat16).reshape(4, 16, depth), LOOP, 0, 0, axis_index_groups=FAR)
    return total(mixed).astype(jnp.bfloat16)


def solution(mesh):
    fine = Mesh(mesh.devices.reshape(4, 2, 2, 2, 2, 2, 4), AXES)
    loop = ("zh", "za", "zb", "xh", "core")
    return jax.shard_map(
        shards,
        mesh=fine,
        in_specs=(P(loop, NARROW), P(NARROW, loop), P(NARROW, loop), P(loop, NARROW)),
        out_specs=P(loop, NARROW),
        check_vma=False,
    )
```

```python
import jax
import jax.numpy as jnp
from jax import lax
from jax.experimental import pallas as pl
from jax.experimental.pallas import tpu as pltpu
from jax.sharding import Mesh, PartitionSpec as P

AXES = ("zh", "za", "zb", "xh", "core", "xl", "y")
NARROW = ("xl", "y")
SWAP = [(0, 1), (1, 0)]
LOOP = ("zh", "za", "zb", "xh", "core")
GROUPS = ((0, 3, 6, 1), (7, 4, 5, 2))


def loop_at(pair, zb, xh, core):
    return (pair + core) % 8 * 8 + zb * 4 + xh * 2 + core


ALONG_Z = [
    [loop_at(pair, zb, xh, core) for pair in range(8) for zb in range(2)]
    for xh in range(2)
    for core in range(2)
]
NEAR = [
    [loop_at(group[at], zb, xh, core) for group in GROUPS for xh in range(2)]
    for at in range(4)
    for zb in range(2)
    for core in range(2)
]
FAR = [
    [loop_at(pair, zb, xh, core) for pair in group]
    for group in GROUPS
    for zb in range(2)
    for xh in range(2)
    for core in range(2)
]
VMEM = pl.BlockSpec(memory_space=pltpu.VMEM)
SMEM = pl.BlockSpec(memory_space=pltpu.SMEM)
HBM = pl.BlockSpec(memory_space=pltpu.HBM)


def total(parts):
    return jnp.sum(parts.astype(jnp.float32), axis=0)


def matmul(a, b, b_dim):
    return lax.dot_general(a, b, (((1,), (b_dim,)), ((), ())), preferred_element_type=jnp.float32)


def project_kernel(slot_ref, x_ref, *refs):
    out_ref, block_ref, sems = refs[-3:]
    weight_refs = refs[:4]
    width = weight_refs[0].shape[0]
    copies = []
    for i, w_ref in enumerate(weight_refs):
        product = matmul(x_ref[...], w_ref[...], 1).astype(out_ref.dtype)
        columns = slice(i * width, (i + 1) * width)
        for at in range(16):
            za = int(at // 2 in GROUPS[1])
            place, zb = GROUPS[za].index(at // 2), at % 2
            block_ref[za, place // 2, zb, place % 2, :, columns] = product[at * 16 : (at + 1) * 16]
        if i % 2:
            half = pl.ds((i - 1) * width, 2 * width)
            copies.append(
                pltpu.make_async_copy(
                    block_ref.at[..., half],
                    out_ref.at[:, slot_ref[0], :, :, :, :, half],
                    sems.at[i // 2],
                )
            )
            copies[-1].start()
    for copy in copies:
        copy.wait()


def hidden_kernel(parts_ref, out_ref):
    width = out_ref.shape[-1]
    totals = parts_ref[0].astype(jnp.float32)
    for i in range(1, parts_ref.shape[0]):
        totals = totals + parts_ref[i].astype(jnp.float32)
    hidden = (jax.nn.silu(totals[..., :width]) * totals[..., width:]).astype(out_ref.dtype)
    for i in range(out_ref.shape[0]):
        out_ref[i] = hidden


def down_kernel(at_zb_ref, hidden_ref, *refs):
    *weight_refs, out_ref, fetched_ref, sems = refs
    width = weight_refs[0].shape[0]
    at_zb = at_zb_ref[0]
    copies = [
        pltpu.make_async_copy(weight_refs[1 + i], fetched_ref.at[i], sems.at[i]) for i in range(2)
    ]
    for copy in copies:
        copy.start()
    mixed = 0.0
    for i in (0, 3, 1, 2):
        side = at_zb if i < 2 else 1 - at_zb
        units = hidden_ref[:, side, :, i % 2 * width : (i % 2 + 1) * width]
        if i in (1, 2):
            copies[i - 1].wait()
        weight = fetched_ref[i - 1] if i in (1, 2) else weight_refs[i][...]
        mixed = mixed + matmul(units.reshape(out_ref.shape[0], width), weight, 0)
    out_ref[...] = mixed.astype(out_ref.dtype)


def call(kernel, specs, out_shape, flops, *args, out_spec=VMEM, scratch=(), aliases={}):
    return pl.pallas_call(
        kernel,
        out_shape=jax.ShapeDtypeStruct(out_shape, jnp.bfloat16),
        in_specs=specs,
        out_specs=out_spec,
        input_output_aliases=aliases,
        scratch_shapes=scratch,
        cost_estimate=pl.CostEstimate(
            flops=flops, bytes_accessed=2 * sum(a.size for a in args), transcendentals=0
        ),
        compiler_params=pltpu.CompilerParams(vmem_limit_bytes=16 << 20),
    )(*args)


def shards(tokens, gate_weight, up_weight, down_weight):
    depth = tokens.shape[1]
    at_xh = lax.axis_index("xh").reshape(1)
    at_zb = lax.axis_index("zb").reshape(1)
    gate, up = gate_weight.T, up_weight.T
    width = gate.shape[0]
    weights = [gate, lax.ppermute(gate, "core", SWAP), up, lax.ppermute(up, "core", SWAP)]

    rows = lax.all_gather(tokens, LOOP, axis=0, tiled=True, axis_index_groups=ALONG_Z)
    n_rows = rows.shape[0]
    other_rows = lax.ppermute(rows, "xh", SWAP)
    flops = 8 * n_rows * depth * width

    def project(slot, x, *started):
        return call(
            project_kernel,
            [SMEM] + [VMEM] * 5 + [HBM] * len(started),
            (2, 2, 2, 2, 2, 16, 4 * width),
            flops,
            slot,
            x,
            *weights,
            *started,
            out_spec=HBM,
            scratch=[
                pltpu.VMEM((2, 2, 2, 2, 16, 4 * width), jnp.bfloat16),
                pltpu.SemaphoreType.DMA((2,)),
            ],
            aliases={6: 0} if started else {},
        )

    partial = project(1 - at_xh, other_rows, project(at_xh, rows))
    down_weight, partial = lax.optimization_barrier((down_weight, partial))
    down_far = lax.ppermute(down_weight, "zb", SWAP)
    down_core = lax.ppermute(down_weight, "core", SWAP)
    parts = lax.all_to_all(partial.reshape(8, 2, 32, 4 * width), NARROW, 0, 0)
    hidden = call(hidden_kernel, [VMEM], (8, 2, 32, 2 * width), 16 * 64 * 4 * width, parts)
    hidden, down_core, down_far = lax.optimization_barrier((hidden, down_core, down_far))
    downs = [down_weight, down_core, down_far, lax.ppermute(down_far, "core", SWAP)]
    hidden = lax.all_to_all(hidden.reshape(16, 32, 2 * width), (*NARROW, "zb"), 0, 0)
    hidden = hidden.reshape(8, 2, 32, 2 * width)
    mixed = call(
        down_kernel,
        [SMEM, VMEM, VMEM, HBM, HBM, VMEM],
        (n_rows, depth),
        8 * n_rows * depth * width,
        at_zb,
        hidden,
        *downs,
        scratch=[
            pltpu.VMEM((2, width, depth), jnp.bfloat16),
            pltpu.SemaphoreType.DMA((2,)),
        ],
    )
    mixed = total(lax.all_to_all(mixed.reshape(4, 64, depth), LOOP, 0, 0, axis_index_groups=NEAR))
    mixed = lax.all_to_all(mixed.astype(jnp.bfloat16).reshape(4, 16, depth), LOOP, 0, 0, axis_index_groups=FAR)
    return total(mixed).astype(jnp.bfloat16)


def solution(mesh):
    fine = Mesh(mesh.devices.reshape(4, 2, 2, 2, 2, 2, 4), AXES)
    loop = ("zh", "za", "zb", "xh", "core")
    return jax.shard_map(
        shards,
        mesh=fine,
        in_specs=(P(loop, NARROW), P(NARROW, loop), P(NARROW, loop), P(loop, NARROW)),
        out_specs=P(loop, NARROW),
        check_vma=False,
    )
```

```python
import jax
import jax.numpy as jnp
from jax import lax
from jax.experimental import pallas as pl
from jax.experimental.pallas import tpu as pltpu
from jax.sharding import Mesh, PartitionSpec as P

AXES = ("zh", "za", "zb", "xh", "core", "xl", "y")
NARROW = ("xl", "y")
FLIPPED = ("y", "xl")
SWAP = [(0, 1), (1, 0)]
LOOP = ("zh", "za", "zb", "xh", "core")
GROUPS = ((0, 3, 6, 1), (7, 4, 5, 2))


def loop_at(pair, zb, xh, core):
    return pair * 8 + zb * 4 + xh * 2 + core


NEAR = [
    [loop_at(group[at], zb, xh, core) for xh in range(2) for group in GROUPS]
    for at in range(4)
    for zb in range(2)
    for core in range(2)
]
FAR = [
    [loop_at(pair, zb, xh, core) for pair in group]
    for group in GROUPS
    for zb in range(2)
    for xh in range(2)
    for core in range(2)
]
VMEM = pl.BlockSpec(memory_space=pltpu.VMEM)
SMEM = pl.BlockSpec(memory_space=pltpu.SMEM)
HBM = pl.BlockSpec(memory_space=pltpu.HBM)


def total(parts):
    return jnp.sum(parts.astype(jnp.float32), axis=0)


def matmul(a, b, b_dim):
    return lax.dot_general(a, b, (((1,), (b_dim,)), ((), ())), preferred_element_type=jnp.float32)


def project_kernel(slot_ref, x_ref, *refs):
    out_ref, block_ref, sems = refs[-3:]
    weight_refs = refs[:4]
    width = weight_refs[0].shape[0]
    copies = []
    for i, w_ref in enumerate(weight_refs):
        product = matmul(x_ref[...], w_ref[...], 1).astype(out_ref.dtype)
        columns = slice(i * width, (i + 1) * width)
        for at in range(16):
            za = int(at // 2 in GROUPS[1])
            place, zb = GROUPS[za].index(at // 2), at % 2
            block_ref[za, place // 2, zb, place % 2, :, columns] = product[at * 16 : (at + 1) * 16]
        if i % 2:
            half = pl.ds((i - 1) * width, 2 * width)
            copies.append(
                pltpu.make_async_copy(
                    block_ref.at[..., half],
                    out_ref.at[slot_ref[0], :, :, :, :, :, half],
                    sems.at[i // 2],
                )
            )
            copies[-1].start()
    for copy in copies:
        copy.wait()


def hidden_kernel(parts_ref, out_ref):
    width = out_ref.shape[-1]
    totals = parts_ref[0].astype(jnp.float32)
    for i in range(1, parts_ref.shape[0]):
        totals = totals + parts_ref[i].astype(jnp.float32)
    hidden = (jax.nn.silu(totals[..., :width]) * totals[..., width:]).astype(out_ref.dtype)
    for i in range(out_ref.shape[0]):
        out_ref[i] = hidden


def down_kernel(at_zb_ref, hidden_ref, *refs):
    *weight_refs, out_ref, fetched_ref, sems = refs
    width = weight_refs[0].shape[0]
    at_zb = at_zb_ref[0]
    copies = [
        pltpu.make_async_copy(weight_refs[1 + i], fetched_ref.at[i], sems.at[i]) for i in range(2)
    ]
    for copy in copies:
        copy.start()
    mixed = 0.0
    for i in (0, 3, 1, 2):
        side = at_zb if i < 2 else 1 - at_zb
        units = hidden_ref[:, side, :, i % 2 * width : (i % 2 + 1) * width]
        if i in (1, 2):
            copies[i - 1].wait()
        weight = fetched_ref[i - 1] if i in (1, 2) else weight_refs[i][...]
        mixed = mixed + matmul(units.reshape(out_ref.shape[0], width), weight, 0)
    out_ref[...] = mixed.astype(out_ref.dtype)


def call(kernel, specs, out_shape, flops, *args, out_spec=VMEM, scratch=(), aliases={}):
    return pl.pallas_call(
        kernel,
        out_shape=jax.ShapeDtypeStruct(out_shape, jnp.bfloat16),
        in_specs=specs,
        out_specs=out_spec,
        input_output_aliases=aliases,
        scratch_shapes=scratch,
        cost_estimate=pl.CostEstimate(
            flops=flops, bytes_accessed=2 * sum(a.size for a in args), transcendentals=0
        ),
        compiler_params=pltpu.CompilerParams(vmem_limit_bytes=16 << 20),
    )(*args)


def shards(tokens, gate_weight, up_weight, down_weight):
    depth = tokens.shape[1]
    at_xh = lax.axis_index("xh").reshape(1)
    at_zb = lax.axis_index("zb").reshape(1)
    gate, up = gate_weight.T, up_weight.T
    width = gate.shape[0]
    weights = [gate, lax.ppermute(gate, "core", SWAP), up, lax.ppermute(up, "core", SWAP)]

    rows = lax.all_gather(tokens, ("zh", "za", "zb"), axis=0, tiled=True)
    n_rows = rows.shape[0]
    other_rows = lax.ppermute(rows, "xh", SWAP)
    flops = 8 * n_rows * depth * width

    def project(slot, x, *started):
        return call(
            project_kernel,
            [SMEM] + [VMEM] * 5 + [HBM] * len(started),
            (2, 2, 2, 2, 2, 16, 4 * width),
            flops,
            slot,
            x,
            *weights,
            *started,
            out_spec=HBM,
            scratch=[
                pltpu.VMEM((2, 2, 2, 2, 16, 4 * width), jnp.bfloat16),
                pltpu.SemaphoreType.DMA((2,)),
            ],
            aliases={6: 0} if started else {},
        )

    partial = project(1 - at_xh, other_rows, project(at_xh, rows))
    down_weight, partial = lax.optimization_barrier((down_weight, partial))
    down_far = lax.ppermute(down_weight, "zb", SWAP)
    down_core = lax.ppermute(down_weight, "core", SWAP)
    parts = lax.all_to_all(partial.reshape(8, 2, 32, 4 * width), FLIPPED, 0, 0)
    hidden = call(hidden_kernel, [VMEM], (8, 2, 32, 2 * width), 16 * 64 * 4 * width, parts)
    hidden, down_core, down_far = lax.optimization_barrier((hidden, down_core, down_far))
    downs = [down_weight, down_core, down_far, lax.ppermute(down_far, "core", SWAP)]
    hidden = lax.all_to_all(hidden.reshape(16, 32, 2 * width), (*FLIPPED, "zb"), 0, 0)
    hidden = hidden.reshape(8, 2, 32, 2 * width)
    mixed = call(
        down_kernel,
        [SMEM, VMEM, VMEM, HBM, HBM, VMEM],
        (n_rows, depth),
        8 * n_rows * depth * width,
        at_zb,
        hidden,
        *downs,
        scratch=[
            pltpu.VMEM((2, width, depth), jnp.bfloat16),
            pltpu.SemaphoreType.DMA((2,)),
        ],
    )
    mixed = total(lax.all_to_all(mixed.reshape(4, 64, depth), LOOP, 0, 0, axis_index_groups=NEAR))
    mixed = lax.all_to_all(mixed.astype(jnp.bfloat16).reshape(4, 16, depth), LOOP, 0, 0, axis_index_groups=FAR)
    return total(mixed).astype(jnp.bfloat16)


def solution(mesh):
    fine = Mesh(mesh.devices.reshape(4, 2, 2, 2, 2, 2, 4), AXES)
    loop = ("zh", "za", "zb", "xh", "core")
    return jax.shard_map(
        shards,
        mesh=fine,
        in_specs=(P(loop, NARROW), P(NARROW, loop), P(NARROW, loop), P(loop, NARROW)),
        out_specs=P(loop, NARROW),
        check_vma=False,
    )
```
